1024 devices in a mesh: rhs: 64 (over z, x), clus: 16 (over y, core).
Axes of the slice: x: 4, y: 8, z: 16, core: 2. Of those that a mesh axis runs over, the one named last changes fastest.
Arguments:
- incident: bfloat16 [6656, 131072], P('rhs', 'clus'), may hold values from -6 to 6
- v_factors: bfloat16 [80, 2048, 128], P('clus', 'rhs'), may hold values from -0.125 to 0.125
- u_factors: bfloat16 [160, 2048, 128], P('clus', 'rhs'), may hold values from -0.5 to 0.5
- block_source: int32 [80], P('clus'), may hold values from 0 to 3
- block_rank: int32 [80], P('clus'), may hold values from 16 to 128
- block_slot: int32 [80], P('clus'), may hold values from 0 to 159, as said below
- slot_target: int32 [160], P('clus'), may hold values from 0 to 3
Outputs:
- scattered: bfloat16 [6656, 131072], P('rhs', 'clus')
The draws below stay inside these ranges and needn't reach their ends.
Inputs may be any that keep to these rules, and one draw needn't show every extreme that they name: `block_slot`: every value is a slot number, all 80 values are distinct, and slot v belongs to index v // 10 of clus. The 5 blocks of one index of clus name at most 1 slots of any one index, and in every draw some index sends exactly 1 to one index and some index of clus receives exactly 10 blocks. Which slots stay empty varies.
All inputs are finite; a program needn't handle non-finite values.
Results may differ from the reference program's by a relative error of at most 0.0049.
Values may be sent and summed in bfloat16 or wider, within the bound.
A program may use at most 64 MiB of HBM per device.

```python
import jax
import jax.numpy as jnp
from jax import lax

CL = 2048
R = 128
CLUS_DEV = 4
BLK_DEV = 5
CLUSTERS = 64
ORDER = 131072
COLS = 6656
NB = 80
RCAP = 10
CAP = 1
N_CLUS = 16


def draw_block_slot(key, part):
    subkeys = jax.random.split(key, 5)
    hottest = jax.random.randint(subkeys[0], (), 0, N_CLUS)
    sequence = jax.random.permutation(subkeys[1], N_CLUS)
    weights = jax.random.randint(subkeys[2], (N_CLUS,), 1, 5)
    slot_scores = jax.random.randint(subkeys[3], (N_CLUS, RCAP), 0, 1 << 20) * RCAP + lax.broadcasted_iota(jnp.int32, (N_CLUS, RCAP), 1)
    shuffles = jnp.argsort(slot_scores, axis=1, stable=True).astype(jnp.int32)
    receiver_ids = jnp.arange(N_CLUS, dtype=jnp.int32)

    def sender_step(sender_turn, state):
        chosen_slots, received = state
        sender = sequence[sender_turn]

        def block_step(block_turn, inner):
            chosen_slots, received, sent_here = inner
            allowed = (sent_here < CAP) & (received < RCAP)
            jitter = jax.random.randint(jax.random.fold_in(subkeys[4], sender_turn * BLK_DEV + block_turn), (N_CLUS,), 0, 1 << 16)
            scores = jnp.where(allowed, jitter * weights * N_CLUS + receiver_ids, -1)
            receiver = jnp.where(allowed[hottest], hottest, jnp.argmax(scores)).astype(jnp.int32)
            slot_value = receiver * RCAP + shuffles[receiver, received[receiver]]
            chosen_slots = chosen_slots.at[sender, block_turn].set(slot_value)
            received = received.at[receiver].add(1)
            sent_here = sent_here.at[receiver].add(1)
            return (chosen_slots, received, sent_here)
        chosen_slots, received, sent_here = lax.fori_loop(0, BLK_DEV, block_step, (chosen_slots, received, jnp.zeros((N_CLUS,), jnp.int32)))
        return (chosen_slots, received)
    chosen_slots, received = lax.fori_loop(0, N_CLUS, sender_step, (jnp.zeros((N_CLUS, BLK_DEV), jnp.int32), jnp.zeros((N_CLUS,), jnp.int32)))
    return chosen_slots.reshape(-1)


def place_ends(array, own_key, least, largest):
    longest = array.shape.index(max(array.shape))
    spots = []
    for shift in (0, 1):
        where = [jax.random.randint(jax.random.fold_in(own_key, axis), (), 0, length) for axis, length in enumerate(array.shape)]
        where[longest] = (where[longest] + shift) % array.shape[longest]
        spots.append(tuple(where))
    return array.at[spots[0]].set(least).at[spots[1]].set(largest)


def block_scale(own_key, shape, pieces, smallest, top_value):
    loudness, own = 1.0, jax.random.fold_in(own_key, 6)
    for dim, parts in pieces:
        heights = jnp.exp(jax.random.uniform(jax.random.fold_in(own, dim), (parts,), jnp.float32, smallest / len(pieces), top_value / len(pieces)))
        loudness = loudness * jnp.repeat(heights, shape[dim] // parts).reshape([-1 if axis == dim else 1 for axis in range(len(shape))])
    return loudness


def centred(own_key, shape, deviation, most, cuts=(), kind=jnp.bfloat16):
    drawn = jax.random.normal(own_key, shape, jnp.float32) * deviation
    if len(cuts) > 0:
        drawn = block_scale(own_key, shape, cuts, -0.22, 0.18) * drawn
    return jnp.clip(drawn, min=-most, max=most).astype(kind)


def setup_inputs(seed: int = 0) -> dict:
    splits = jax.random.split(jax.random.key(seed), 8)
    return {
        "incident": centred(splits[0], (COLS, ORDER), 1.0, 6.0, ((0, 64), (1, 16))),
        "v_factors": centred(splits[1], (NB, CL, R), CL ** -0.5, 0.125, ((0, 16), (1, 64))),
        "u_factors": centred(splits[2], (N_CLUS * RCAP, CL, R), R ** -0.5, 0.5, ((0, 16), (1, 64))),
        "block_source": place_ends(jax.random.randint(splits[3], (NB,), 0, CLUS_DEV), jax.random.fold_in(splits[3], 1), 0, CLUS_DEV - 1).astype(jnp.int32),
        "block_rank": place_ends(jax.random.randint(splits[4], (NB,), R // 8, R + 1), jax.random.fold_in(splits[4], 1), R // 8, R).astype(jnp.int32),
        "block_slot": draw_block_slot(jax.random.fold_in(splits[7], 71), 0),
        "slot_target": place_ends(jax.random.randint(splits[6], (N_CLUS * RCAP,), 0, CLUS_DEV), jax.random.fold_in(splits[6], 1), 0, CLUS_DEV - 1).astype(jnp.int32),
    }


def reference(incident, v_factors, u_factors, block_source, block_rank, block_slot, slot_target):
    columns = incident.shape[0]
    sources = incident.reshape(columns, CLUSTERS, CL)
    rank_range = jnp.arange(R, dtype=jnp.int32)

    def project(block_index):
        cluster = (block_index // BLK_DEV) * CLUS_DEV + block_source[block_index]
        window = lax.dynamic_index_in_dim(sources, cluster, axis=1, keepdims=False)
        product = jnp.dot(window, v_factors[block_index], preferred_element_type=jnp.float32)
        masked = jnp.where(rank_range[None, :] < block_rank[block_index], product, jnp.zeros_like(product))
        return masked.astype(jnp.bfloat16)

    compressed = lax.map(project, jnp.arange(NB, dtype=jnp.int32))
    slot_rows = jnp.zeros((N_CLUS * RCAP, columns, R), jnp.bfloat16).at[block_slot].set(compressed)
    cluster_range = jnp.arange(CLUS_DEV, dtype=jnp.int32)

    def expand(device):
        def add_slot(running, local_slot):
            slot_index = device * RCAP + local_slot
            product = jnp.dot(slot_rows[slot_index], u_factors[slot_index].T, preferred_element_type=jnp.float32)
            owner = (cluster_range == slot_target[slot_index]).astype(jnp.float32)
            return running + owner[None, :, None] * product[:, None, :], None

        running, _unused = lax.scan(add_slot, jnp.zeros((columns, CLUS_DEV, CL), jnp.float32), jnp.arange(RCAP, dtype=jnp.int32))
        return running.astype(jnp.bfloat16)

    per_device = lax.map(expand, jnp.arange(N_CLUS, dtype=jnp.int32))
    return jnp.transpose(per_device, (1, 0, 2, 3)).reshape(columns, ORDER)
```

```python
import functools

import jax
import jax.numpy as jnp
from jax import lax
from jax.experimental import pallas as pl
from jax.experimental.pallas import tpu as pltpu
from jax.sharding import Mesh
from jax.sharding import PartitionSpec as P

MESH = pl.DeviceIdType.MESH
NZ, NX, NC = 16, 4, 16
HALF = NZ // 2
BLOCKS, SLOTS, CLUSTERS = 5, 10, 4
COLS, ROWS, R, CL = 104, 32, 128, 2048
GROUP = NX * ROWS
PAD = 112
V_PARTS, V_A = ((0, 1),), 1
U_PARTS, U_A = ((0, 1), (1, 2), (2, 3), (3, 4), (4, 5)), 5
PER_HOP, SELECT_AT = 3, 5
V_LAG, U_LAG = 3, 2


def schedule():
    flow = [("UX", 0, 0)]
    for s in range(HALF + 1):
        flow += [("U", s, i) for i in range(len(U_PARTS))]
        if s > 0:
            flow.append(("U", s, -1))
        if s > U_LAG:
            flow.append(("X", s - U_LAG, 0))
    flow += [("X", s, 0) for s in range(HALF - U_LAG + 1, HALF + 1)]
    ops = [("V0", 0, 0), ("U0", 0, 0), ("VX", 0, 0)]
    for h in range(1, HALF + 1):
        ops += [("V", h, i) for i in (*range(len(V_PARTS)), -1)]
        ops, flow = ops + flow[:PER_HOP], flow[PER_HOP:]
        ops += [("W", h - V_LAG, 0)] if h > V_LAG else []
        ops += [("G", 0, 0)] if h == 2 else []
        ops += [("P", h - V_LAG - 2, 0)] if h > V_LAG + 2 else []
    for h in range(HALF - V_LAG + 1, HALF + 1):
        ops += [("W", h, 0), *flow[:2], ("P", h - 2, 0)]
        flow = flow[2:]
    ops += [("P", HALF - 1, 0), *flow[:1], ("P", HALF, 0), ("C", 0, 0)]
    flow = flow[1:]
    ready = 0
    chosen = False
    for op in (*flow, ("END", 0, 0)):
        kind, s, i = op
        if not chosen and (kind == "END" or (kind == "X" and s == SELECT_AT)):
            ops += [("L", 0, 0), ("S", 0, 0)]
            chosen = True
        if kind == "END":
            ops += [("E", e, 0) for e in range(ready + 1, HALF + 1)]
            break
        ops.append(op)
        if chosen and kind == "X":
            upto = s - 1
            ops += [("E", e, 0) for e in range(ready + 1, upto + 1)]
            ready = max(ready, upto)
    return ops


PEERS = (8, 7, 9, 6, 10, 5, 11, 4, 12, 3, 13, 2, 14, 1, 15)


class Names:
    def __init__(self):
        self.number = {}

    def __call__(self, *name):
        return self.number.setdefault(name, len(self.number))


def kernel(
    x_hbm, v_hbm, u_hbm, source_hbm, rank_hbm, slot_hbm, target_hbm, out_hbm,
    x_ref, windows, gv, gu, acc, packed, outgoing, arrived, left, out_ref, mine, theirs,
    to_window, to_peer, to_slot, to_owner, source, rank, slot, target, recv, send, local, store,
):
    z, x, c = lax.axis_index("rhs_0"), lax.axis_index("rhs_1"), lax.axis_index("clus")
    up, down = {"rhs_0": lax.rem(z + 1, NZ)}, {"rhs_0": lax.rem(z + NZ - 1, NZ)}
    side = {k: {"rhs_1": lax.rem(x + k, NX)} for k in (1, 2, 3)}
    peer = {k: {"clus": lax.rem(c + k, NC)} for k in range(1, NC)}
    number = Names()
    sent, stores, early = [], [], []

    def remote(name, src, dst, device):
        i = number(*name)
        return pltpu.make_async_remote_copy(
            src_ref=src,
            dst_ref=dst,
            send_sem=send.at[i],
            recv_sem=recv.at[i],
            device_id=device,
            device_id_type=MESH,
        )

    def push(name, src, dst, device):
        copy = remote(name, src, dst, device)
        copy.start()
        sent.append(copy)

    def drain(last):
        while len(early) < last:
            sent[len(early)].wait_send()
            early.append(True)

    def landed(name, dst):
        remote(name, dst, dst, up).wait_recv()

    def rows(k, start=0, size=ROWS):
        first = lax.rem(x + k, NX) * ROWS + start
        return pl.ds(pl.multiple_of(first, 16), size)

    x_copies = [
        pltpu.make_async_copy(
            x_hbm.at[:, t * CL : (t + 1) * CL], x_ref.at[t, :COLS, :], local.at[9 + t]
        )
        for t in range(CLUSTERS)
    ]
    v_copy = pltpu.make_async_copy(v_hbm, gv.at[0, :, rows(0), :], local.at[1])
    u_copy = pltpu.make_async_copy(u_hbm, gu.at[0, :, rows(0), :], local.at[2])
    small = [
        pltpu.make_async_copy(a, b, local.at[3 + i])
        for i, (a, b) in enumerate(
            ((slot_hbm, slot), (source_hbm, source), (rank_hbm, rank), (target_hbm, target))
        )
    ]
    for copy in (*small, v_copy, u_copy, *x_copies):
        copy.start()

    barrier = pltpu.get_barrier_semaphore()
    partners = [up, down, *side.values(), *peer.values()]
    for device in partners:
        pl.semaphore_signal(barrier, inc=1, device_id=device, device_id_type=MESH)
    for t in range(CLUSTERS):
        x_ref[t, COLS:, :] = jnp.zeros((PAD - COLS, CL), jnp.bfloat16)
    for k in range(NC):
        arrived[k, COLS:, :] = jnp.zeros((PAD - COLS, R), jnp.bfloat16)
    pl.semaphore_wait(barrier, len(partners))

    streams = {
        "V": (gv, v_hbm, BLOCKS, V_PARTS, V_A),
        "U": (gu, u_hbm, SLOTS, U_PARTS, U_A),
    }

    def begin(f):
        full, own, count, _, cut = streams[f]
        for k in (1, 3, 2):
            push((f, "x0", k), own, full.at[0, :, rows(0), :], side[k])
        push((f, "z+", 1, -1), own.at[cut:], full.at[NZ - 1, cut:, rows(0), :], up)
        push((f, "z-", 1, -1), own.at[cut:], full.at[1, cut:, rows(0), :], down)

    def begin_x(f):
        full, _, _, _, _ = streams[f]
        for k in (1, 3, 2):
            landed((f, "x0", k), full.at[0, :, rows(NX - k), :])

    def spread(f, d):
        full, _, _, _, cut = streams[f]
        for k in (1, 3):
            ref = full.at[d, cut:, rows(0), :]
            push((f, "x", d, k), ref, ref, side[k])

    def step(f, s, i):
        full, _, _, parts, cut = streams[f]
        last, following = s == HALF, s + 1 == HALF
        for sign in "+-":
            d = (NZ - s if sign == "+" else s) % NZ
            onward = (NZ - s - 1 if sign == "+" else s + 1) % NZ
            device = up if sign == "+" else down
            half = 0 if sign == "+" else 1

            def place(part):
                if i >= 0:
                    size = GROUP // 2 if part else GROUP
                    return slice(*parts[i]), pl.ds(half * size if part else 0, size)
                return slice(cut, None), (rows(0, half * (ROWS // 2), ROWS // 2) if part else rows(0))

            if s > 0:
                landed((f, "z" + sign, s, i), full.at[(d, *place(last))])
            if not last:
                push(
                    (f, "z" + sign, s + 1, i),
                    full.at[(d, *place(following))],
                    full.at[(onward, *place(following))],
                    device,
                )
                if i < 0:
                    spread(f, d)
        if last and i < 0:
            spread(f, HALF)

    def pair(s):
        return (HALF,) if s == HALF else (NZ - s, s)

    def sideways(f, s):
        full, _, _, _, cut = streams[f]
        for d in pair(s):
            for k, half in ((1, 0), (3, 1)):
                landed((f, "x", d, k), full.at[d, cut:, rows(NX - k), :])
                ref = full.at[d, cut:, rows(NX - k, half * (ROWS // 2), ROWS // 2), :]
                push((f, "far", d, k), ref, ref, side[k])

    def complete(f, s):
        full, _, _, _, cut = streams[f]
        for d in pair(s):
            for k, half in ((1, 0), (3, 1)):
                ref = full.at[d, cut:, rows(2, half * (ROWS // 2), ROWS // 2), :]
                landed((f, "far", d, k), ref)

    def column(d):
        return lax.rem(z + d, NZ) * GROUP

    def one_hot(value, wanted):
        hit = jnp.full((16, 128), value, jnp.int32) == wanted
        return jnp.where(hit, 1.0, 0.0).astype(jnp.bfloat16)

    def make_labels():
        for copy in small:
            copy.wait()
        for k in range(NC):
            label = jnp.full((16, 128), -1, jnp.int32)
            for b in range(BLOCKS):
                device = jnp.full((16, 128), lax.div(slot[b], SLOTS), jnp.int32)
                place = jnp.full((16, 128), lax.rem(slot[b], SLOTS), jnp.int32)
                label = jnp.where(device == lax.rem(c + k, NC), place, label)
            if k == 0:
                theirs[0] = label
            else:
                mine[k] = label

    def tables():
        for b in range(BLOCKS):
            for t in range(CLUSTERS):
                to_window[b * CLUSTERS + t] = one_hot(source[b], t)
        for b in range(BLOCKS):
            device = lax.div(slot[b], SLOTS)
            for k in range(NC):
                to_peer[k * BLOCKS + b] = one_hot(device, lax.rem(c + k, NC))
        for j in range(SLOTS):
            for t in range(CLUSTERS):
                to_owner[j * CLUSTERS + t] = one_hot(target[j], t)

    def mix(weights, first, tiles):
        total = None
        for i, tile in enumerate(tiles):
            term = weights[first + i] * tile
            total = term if total is None else total + term
        return total

    def compress(s):
        complete("V", s)
        one, two = (0, HALF) if s == HALF else (NZ - s, s)
        places = [pl.ds(pl.multiple_of(column(d), GROUP), GROUP) for d in (one, two)]

        @pl.loop(0, PAD // 16)
        def _(i):
            row = pl.ds(pl.multiple_of(i * 16, 16), 16)
            for n, place in enumerate(places):
                tiles = [x_ref[t, row, place] for t in range(CLUSTERS)]
                for b in range(BLOCKS):
                    windows[b, row, n * GROUP : (n + 1) * GROUP] = mix(to_window, b * CLUSTERS, tiles)

        for b in range(BLOCKS):
            factor = jnp.concatenate([gv[one, b], gv[two, b]], axis=0)
            product = jnp.dot(windows[b], factor, preferred_element_type=jnp.float32)
            acc[b] = product if s == 1 else acc[b] + product

    def dispatch():
        k_index = lax.broadcasted_iota(jnp.int32, (PAD, R), 1)
        for b in range(BLOCKS):
            packed[b] = jnp.where(k_index < rank[b], acc[b], 0.0).astype(jnp.bfloat16)

        @pl.loop(0, PAD // 16)
        def _(i):
            row = pl.ds(pl.multiple_of(i * 16, 16), 16)
            tiles = [packed[b, row, :] for b in range(BLOCKS)]
            for k in range(1, NC):
                outgoing[k, row, :] = mix(to_peer, k * BLOCKS, tiles)
            arrived[0, row, :] = mix(to_peer, 0, tiles)

        for k in PEERS:
            push(("rows", k), outgoing.at[k, :COLS, :], arrived.at[k, :COLS, :], peer[k])

    def read_labels():
        for k in PEERS:
            landed(("label", k), theirs.at[k])
        for k in range(NC):
            label = theirs[k]
            for j in range(SLOTS):
                to_slot[j * NC + k] = jnp.where(label == j, 1.0, 0.0).astype(jnp.bfloat16)

    def select():
        for k in PEERS:
            landed(("rows", k), arrived.at[k, :COLS, :])

        @pl.loop(0, PAD // 16)
        def _(i):
            row = pl.ds(pl.multiple_of(i * 16, 16), 16)
            tiles = [arrived[k, row, :] for k in range(NC)]
            for j in range(SLOTS):
                values = mix(to_slot, j * NC, tiles)
                for t in range(CLUSTERS):
                    place = pl.ds(pl.multiple_of(t * PAD + i * 16, 16), 16)
                    left[place, j * R : (j + 1) * R] = to_owner[j * CLUSTERS + t] * values

    def expand(s):
        complete("U", s)
        one, two = (0, HALF) if s == HALF else (NZ - s, s)
        total = None
        for j in range(0, SLOTS, 2):
            right = jnp.concatenate(
                [jnp.concatenate([gu[d, j], gu[d, j + 1]], axis=1) for d in (one, two)], axis=0
            )
            product = lax.dot_general(
                left[:, j * R : (j + 2) * R],
                right,
                (((1,), (1,)), ((), ())),
                preferred_element_type=jnp.float32,
            )
            total = product if total is None else total + product
        rounded = total.astype(jnp.bfloat16)
        for t in range(CLUSTERS):
            for i, d in enumerate((one, two)):
                place = pl.ds(pl.multiple_of(t * CL + column(d), GROUP), GROUP)
                out_ref[:, place] = rounded[t * PAD : t * PAD + COLS, i * GROUP : (i + 1) * GROUP]
                copy = pltpu.make_async_copy(
                    out_ref.at[:, place], out_hbm.at[:, place], store.at[(s - 1) * 8 + t * 2 + i]
                )
                copy.start()
                stores.append(copy)

    marks = []
    for kind, s, i in schedule():
        if kind == "V0":
            begin("V")
            make_labels()
        elif kind == "U0":
            begin("U")
        elif kind == "VX":
            v_copy.wait()
            begin_x("V")
            for p in range(len(V_PARTS)):
                step("V", 0, p)
            for k in PEERS:
                push(("label", k), mine.at[k], theirs.at[k], peer[k])
            tables()
        elif kind == "UX":
            u_copy.wait()
            begin_x("U")
        elif kind == "G":
            for copy in x_copies:
                copy.wait()
        elif kind in "VU":
            step(kind, s, i)
        elif kind == "W":
            sideways("V", s)
        elif kind == "X":
            sideways("U", s)
        elif kind == "P":
            compress(s)
        elif kind == "C":
            dispatch()
            marks.insert(0, len(sent))
        elif kind == "L":
            read_labels()
            drain(marks[0] - len(PEERS))
        elif kind == "S":
            select()
        elif kind == "E":
            expand(s)
            if len(marks) > 1:
                drain(marks.pop(1))
        if kind == "X":
            marks.append(len(sent) - 12)
    drain(len(sent))
    for one in stores:
        one.wait()


COPIES = 2 * (3 + 2 * 8 + 15 * 4) + 16 * (len(V_PARTS) + len(U_PARTS)) + 30


def local(incident, v_factors, u_factors, block_source, block_rank, block_slot, slot_target):
    anywhere, outside = pl.BlockSpec(memory_space=pl.ANY), pl.BlockSpec(memory_space=pltpu.HBM)
    return pl.pallas_call(
        kernel,
        out_shape=jax.ShapeDtypeStruct(incident.shape, jnp.bfloat16),
        in_specs=[outside] * 7,
        out_specs=anywhere,
        scratch_shapes=[
            pltpu.VMEM((CLUSTERS, PAD, CL), jnp.bfloat16),
            pltpu.VMEM((BLOCKS, PAD, 2 * GROUP), jnp.bfloat16),
            pltpu.VMEM((NZ, BLOCKS, GROUP, R), jnp.bfloat16),
            pltpu.VMEM((NZ, SLOTS, GROUP, R), jnp.bfloat16),
            pltpu.VMEM((BLOCKS, PAD, R), jnp.float32),
            pltpu.VMEM((BLOCKS, PAD, R), jnp.bfloat16),
            pltpu.VMEM((NC, PAD, R), jnp.bfloat16),
            pltpu.VMEM((NC, PAD, R), jnp.bfloat16),
            pltpu.VMEM((CLUSTERS * PAD, SLOTS * R), jnp.bfloat16),
            pltpu.VMEM((COLS, CLUSTERS * CL), jnp.bfloat16),
            pltpu.VMEM((NC, 16, 128), jnp.int32),
            pltpu.VMEM((NC, 16, 128), jnp.int32),
            pltpu.VMEM((BLOCKS * CLUSTERS, 16, 128), jnp.bfloat16),
            pltpu.VMEM((NC * BLOCKS, 16, 128), jnp.bfloat16),
            pltpu.VMEM((SLOTS * NC, 16, 128), jnp.bfloat16),
            pltpu.VMEM((SLOTS * CLUSTERS, 16, 128), jnp.bfloat16),
            pltpu.SMEM((BLOCKS,), jnp.int32),
            pltpu.SMEM((BLOCKS,), jnp.int32),
            pltpu.SMEM((BLOCKS,), jnp.int32),
            pltpu.SMEM((SLOTS,), jnp.int32),
            pltpu.SemaphoreType.DMA((COPIES,)),
            pltpu.SemaphoreType.DMA((COPIES,)),
            pltpu.SemaphoreType.DMA((13,)),
            pltpu.SemaphoreType.DMA((64,)),
        ],
        compiler_params=pltpu.CompilerParams(
            collective_id=0, has_side_effects=True, vmem_limit_bytes=60 * 1024 * 1024
        ),
        name="far_field",
    )(incident, v_factors, u_factors, block_source, block_rank, block_slot, slot_target)


def solution(mesh):
    torus = Mesh(mesh.devices.reshape(NZ, NX, NC), ("rhs_0", "rhs_1", "clus"))
    rhs = ("rhs_0", "rhs_1")
    return jax.shard_map(
        local,
        mesh=torus,
        in_specs=(
            P(rhs, "clus"),
            P("clus", rhs, None),
            P("clus", rhs, None),
            P("clus"),
            P("clus"),
            P("clus"),
            P("clus"),
        ),
        out_specs=P(rhs, "clus"),
        check_vma=False,
    )
```
